32 devices in a mesh: scen: 8 (over z, y), area: 4 (over x, core).
Axes of the slice: x: 2, y: 2, z: 4, core: 2. Of those that a mesh axis runs over, the one named last changes fastest.
Arguments:
- wind: bfloat16 [8, 24, 24576], P('scen', None, 'area'), may hold values from -4 to 4
- load: bfloat16 [24, 24576], P(None, 'area'), may hold values from 0 to 1.5
- ptdf_tiles: bfloat16 [128, 32, 128, 128], P('area'), may hold values from -0.09375 to 0.09375
- tile_cols: int32 [128, 32], P('area'), may hold values from 0 to 191, as said below
- line_cap: float32 [16384], P('area'), may hold values from 0.3 to 3
- gen_bus: int32 [4096], P('area'), may hold values from 0 to 24575, as said below
- gen_data: float32 [4, 4096], P(None, 'area'), may hold values from 0.05 to 18, as said below
- prob_weight: int32 [8], P('scen'), may hold values from 1 to 16
Outputs:
- commit_mean: float32 [24, 4096], P(None, 'area')
- dispatch_mean: float32 [24, 4096], P(None, 'area')
- dispatch: float32 [8, 24, 4096], P('scen', None, 'area')
- line_flow: float32 [8, 24, 16384], P('scen', None, 'area')
The draws below stay inside these ranges and needn't reach their ends.
Inputs may be any that keep to these rules, and one draw needn't show every extreme that they name: `tile_cols`: the 32 bus tiles of one row of line tiles are distinct. `gen_bus`: generator g stands at a bus of area g // 1024, that is among buses (g // 1024) * 6144 to (g // 1024 + 1) * 6144 - 1. `gen_data`: linear cost 0.5 to 2, quadratic cost 0.05 to 0.5, commitment cost 0.2 to 1, capacity 2 to 18.
All inputs are finite; a program needn't handle non-finite values.
Results may differ from the reference program's by a relative error of at most 0.003.
Values may be sent and summed in bfloat16 or wider, within the bound.
A program may use at most 128 MiB of HBM per device.

```python
import math
import jax
import jax.numpy as jnp
from jax import lax

BUSES = 24576
LINES = 16384
GENS = 4096
HOURS = 24
TILE = 128
NZ = 32
ITERS = 2
STEPS = 2
SCENS = 8
B_DEV = 6144
G_DEV = 1024
N_AREA = 4


def draw_tile_cols(key, part):
    bus_tiles = BUSES // TILE
    row_keys = jax.random.split(jax.random.fold_in(key, 11), LINES // TILE)
    orders = jax.vmap(lambda subkey: jax.random.permutation(subkey, bus_tiles))(row_keys)
    return orders[:, :NZ].astype(jnp.int32)


def draw_gen_bus(key, part):
    owner = jnp.arange(GENS, dtype=jnp.int32) // G_DEV
    offset = jax.random.randint(jax.random.fold_in(key, 23), (GENS,), 0, B_DEV).astype(jnp.int32)
    offset = offset.at[0].set(0).at[GENS - 1].set(B_DEV - 1)
    return (owner * B_DEV + offset).astype(jnp.int32)


def draw_gen_data(key, part):
    keys = jax.random.split(jax.random.fold_in(key, 37), 4)
    linear = jax.random.uniform(keys[0], (GENS,), jnp.float32, 0.5, 2.0)
    quadratic = jnp.exp(jax.random.uniform(keys[1], (GENS,), jnp.float32, jnp.log(0.05), jnp.log(0.5)))
    fixed_cost = jax.random.uniform(keys[2], (GENS,), jnp.float32, 0.2, 1.0)
    capacity = jnp.exp(jax.random.uniform(keys[3], (GENS,), jnp.float32, jnp.log(2.0), jnp.log(18.0)))
    return jnp.stack([linear, quadratic, fixed_cost, capacity]).astype(jnp.float32)


def touch_ends(values, stream_key, smallest, high):
    place = [jax.random.randint(jax.random.fold_in(stream_key, axis), (), 0, length) for axis, length in enumerate(values.shape)]
    longest = values.shape.index(max(values.shape))
    next_to = place[:longest] + [(place[longest] + 1) % values.shape[longest]] + place[longest + 1:]
    return values.at[tuple(place)].set(smallest).at[tuple(next_to)].set(high)


def level_of(own_key, shape, cuts, low, top_value):
    def one(position, shards_of):
        draws = jax.random.uniform(jax.random.fold_in(jax.random.fold_in(own_key, 6), position), (shards_of,), jnp.float32, low / len(cuts), top_value / len(cuts))
        return jnp.repeat(jnp.exp(draws), shape[position] // shards_of).reshape((-1,) + (1,) * (len(shape) - position - 1))

    level = one(*cuts[0])
    for cut in cuts[1:]:
        level = level * one(*cut)
    return level


def scatter_about(key, shape, scale, limit, cuts=(), held_as=jnp.bfloat16):
    level = level_of(key, shape, cuts, -0.22, 0.18) if cuts else 1.0
    entries = jax.random.normal(key, shape, jnp.float32) * scale * level
    return jnp.minimum(jnp.maximum(entries, -limit), limit).astype(held_as)


def setup_inputs(seed: int = 0) -> dict:
    key_of = jax.random.split(jax.random.key(seed), 9)
    return {
        "wind": scatter_about(key_of[0], (SCENS, HOURS, BUSES), 0.5, 4.0, ((0, 8), (2, 4))),
        "load": jnp.clip(1.5 * jax.random.uniform(key_of[1], (HOURS, BUSES), jnp.float32) ** level_of(key_of[1], (HOURS, BUSES), ((1, 4),), -0.2, 0.2), 0.0, 1.5).astype(jnp.bfloat16),
        "ptdf_tiles": scatter_about(key_of[2], (LINES // TILE, NZ, TILE, TILE), (NZ * TILE) ** -0.5, 0.09375, ((0, 4),)),
        "tile_cols": draw_tile_cols(jax.random.fold_in(key_of[8], 71), 0),
        "line_cap": jnp.clip(jnp.exp(math.log(3.0) - 2.3025851 * jax.random.uniform(key_of[4], (LINES,), jnp.float32) ** level_of(key_of[4], (LINES,), ((0, 4),), -0.2, 0.2)), 0.3, 3.0),
        "gen_bus": draw_gen_bus(jax.random.fold_in(key_of[8], 71), 0),
        "gen_data": draw_gen_data(jax.random.fold_in(key_of[8], 71), 0),
        "prob_weight": touch_ends(jax.random.randint(key_of[7], (SCENS,), 1, 17), jax.random.fold_in(key_of[7], 1), 1, 16).astype(jnp.int32),
    }


penalty = 1.0
flow_weight = 0.25
commit_step = 0.5


def rounded(values):
    return lax.optimization_barrier(values.astype(jnp.bfloat16)).astype(jnp.float32)


def scenario_steps(state, load, ptdf_wide, tile_cols, line_cap, gen_bus, gen_data, comm_mean, disp_mean):
    dispatch, commit, w_disp, w_comm, wind_s = state
    linear, quadratic, fixed_cost, capacity = gen_data[0], gen_data[1], gen_data[2], gen_data[3]
    step_gen = 1.0 / (quadratic + penalty + 2.0)
    bus_tiles = BUSES // TILE
    line_tiles = LINES // TILE
    lt_dev = line_tiles // N_AREA
    flow = jnp.zeros((HOURS, LINES), jnp.float32)
    for step_index in range(STEPS):
        placed = jax.ops.segment_sum(dispatch.T, gen_bus, num_segments=BUSES).T
        injection = (placed + wind_s.astype(jnp.float32) - load.astype(jnp.float32)).astype(jnp.bfloat16)
        inj_f = injection.astype(jnp.float32)
        picked = inj_f.reshape(HOURS, bus_tiles, TILE)[:, tile_cols]
        flow = jnp.einsum("hkzb,kzlb->hkl", picked, ptdf_wide).reshape(HOURS, LINES)
        excess = flow - jnp.clip(flow, -line_cap, line_cap)
        imbalance = jnp.sum(inj_f, axis=1)
        ex_b = rounded(excess).reshape(HOURS, line_tiles, TILE)
        contrib = jnp.einsum("hkl,kzlb->hkzb", ex_b, ptdf_wide)
        contrib = contrib.reshape(HOURS, N_AREA, lt_dev, NZ, TILE)
        area_idx = jnp.arange(N_AREA, dtype=jnp.int32)[:, None, None]
        cols_r = tile_cols.reshape(N_AREA, lt_dev, NZ)
        partial_value = jnp.zeros((HOURS, N_AREA, bus_tiles, TILE), jnp.float32).at[:, area_idx, cols_r].add(contrib)
        price = jnp.sum(rounded(partial_value), axis=1).reshape(HOURS, BUSES)
        grad = linear + quadratic * dispatch + flow_weight * price[:, gen_bus] + imbalance[:, None] / BUSES + w_disp + penalty * (dispatch - disp_mean)
        commit = jnp.clip(commit - commit_step * (fixed_cost - dispatch / capacity + w_comm + penalty * (commit - comm_mean)), 0.0, 1.0)
        dispatch = jnp.clip(dispatch - step_gen * grad, 0.0, capacity * commit)
    return dispatch, commit, flow


def reference(wind, load, ptdf_tiles, tile_cols, line_cap, gen_bus, gen_data, prob_weight):
    weights = prob_weight.astype(jnp.float32)
    prob = weights / jnp.sum(weights)
    capacity = gen_data[3]
    ptdf_wide = ptdf_tiles.astype(jnp.float32)
    commit = jnp.full((SCENS, HOURS, GENS), 0.5, jnp.float32)
    dispatch = jnp.zeros((SCENS, HOURS, GENS), jnp.float32) + 0.25 * capacity
    comm_mean = jnp.full((HOURS, GENS), 0.5, jnp.float32)
    disp_mean = jnp.zeros((HOURS, GENS), jnp.float32) + 0.25 * capacity
    w_comm = jnp.zeros((SCENS, HOURS, GENS), jnp.float32)
    w_disp = jnp.zeros((SCENS, HOURS, GENS), jnp.float32)
    flows = jnp.zeros((SCENS, HOURS, LINES), jnp.float32)
    for round_index in range(ITERS):
        def one_scenario(state):
            return scenario_steps(state, load, ptdf_wide, tile_cols, line_cap, gen_bus, gen_data, comm_mean, disp_mean)
        dispatch, commit, flows = lax.map(one_scenario, (dispatch, commit, w_disp, w_comm, wind))
        comm_mean = jnp.sum(prob[:, None, None] * commit, axis=0)
        disp_mean = jnp.sum(prob[:, None, None] * dispatch, axis=0)
        w_comm = w_comm + penalty * (commit - comm_mean)
        w_disp = w_disp + penalty * (dispatch - disp_mean)
    return comm_mean, disp_mean, dispatch, flows
```

```python
import functools
import jax
import jax.numpy as jnp
from jax import lax
from jax.experimental import pallas as pl
from jax.experimental.pallas import tpu as pltpu
from jax.sharding import PartitionSpec as P

ITERS = 2
STEPS = 2

penalty = 1.0
flow_weight = 0.25
commit_step = 0.5

SPAN = 8
NT = (((1,), (1,)), ((), ()))
HIGH = lax.Precision.HIGHEST


def flow_kernel(cols_sm, lo_sm, hi_sm, inj, w, cap, bus, flow, price, imb, acc):
    step = pl.program_id(0)
    block, slots, tile, _ = w.shape
    tiles = inj.shape[0]

    @pl.when(step == 0)
    def _():
        acc[...] = jnp.zeros_like(acc)

        def add(t, sums):
            return tuple(s + inj[t * 4 + i].astype(jnp.float32) for i, s in enumerate(sums))

        zero = jnp.zeros(imb.shape, jnp.float32)
        parts = lax.fori_loop(0, tiles // 4, add, (zero,) * 4)
        total = parts[0] + parts[1] + parts[2] + parts[3]
        imb[...] = jnp.broadcast_to(jnp.sum(total, axis=1, keepdims=True), imb.shape)

    flows = []
    cols = []
    for kk in range(block):
        base = (step * block + kk) * slots
        own = [cols_sm[base + z] for z in range(slots)]
        picked = jnp.concatenate([inj[c] for c in own], axis=1)
        wide = jnp.concatenate([w[kk, z] for z in range(slots)], axis=1)
        flows.append(lax.dot_general(picked, wide, NT, preferred_element_type=jnp.float32))
        cols.append(own)
    contribs = []
    for kk in range(block):
        value = flows[kk]
        flow[:, kk * tile:(kk + 1) * tile] = value
        limit = cap[0, :, kk * tile:(kk + 1) * tile]
        excess = (value - jnp.clip(value, -limit, limit)).astype(jnp.bfloat16)
        wide = jnp.concatenate([w[kk, z] for z in range(slots)], axis=1)
        contribs.append(jnp.dot(excess, wide, preferred_element_type=jnp.float32))
    for kk in range(block):
        for z in range(slots):
            c = cols[kk][z]
            acc[c] = acc[c] + contribs[kk][:, z * tile:(z + 1) * tile]

    @pl.when(step == pl.num_programs(0) - 1)
    def _():
        def one(j, carry):
            where = jnp.broadcast_to(bus[j], imb.shape)
            own_tile = where // tile
            lane = where - own_tile * tile

            def pick(t, found):
                values = acc[t].astype(jnp.bfloat16).astype(jnp.float32)
                got = jnp.take_along_axis(values, lane, axis=1, mode="promise_in_bounds")
                return jnp.where(own_tile == t, got, found)

            found = jnp.zeros(imb.shape, jnp.float32)
            low = lo_sm[j]
            for i in range(SPAN):
                found = pick(jnp.minimum(low + i, tiles - 1), found)
            found = lax.fori_loop(low + SPAN, hi_sm[j] + 1, pick, found)
            price[j] = found.astype(jnp.bfloat16)
            return carry

        lax.fori_loop(0, bus.shape[0], one, 0)


def flows_and_prices(inj, w, cols, cap, bus, low, high, block=2):
    tiles, rows, tile = inj.shape
    lines, slots = w.shape[0], w.shape[1]
    block = block if lines % block == 0 else 1
    groups = bus.shape[0]
    return pl.pallas_call(
        flow_kernel,
        grid_spec=pltpu.PrefetchScalarGridSpec(
            num_scalar_prefetch=3,
            grid=(lines // block,),
            in_specs=[
                pl.BlockSpec((tiles, rows, tile), lambda k, *_: (0, 0, 0)),
                pl.BlockSpec((block, slots, tile, tile), lambda k, *_: (k, 0, 0, 0)),
                pl.BlockSpec((1, 1, block * tile), lambda k, *_: (k, 0, 0)),
                pl.BlockSpec((groups, 1, tile), lambda k, *_: (0, 0, 0)),
            ],
            out_specs=[
                pl.BlockSpec((rows, block * tile), lambda k, *_: (0, k)),
                pl.BlockSpec((groups, rows, tile), lambda k, *_: (0, 0, 0)),
                pl.BlockSpec((rows, tile), lambda k, *_: (0, 0)),
            ],
            scratch_shapes=[pltpu.VMEM((tiles, rows, tile), jnp.float32)],
        ),
        out_shape=[
            jax.ShapeDtypeStruct((rows, lines * tile), jnp.float32),
            jax.ShapeDtypeStruct((groups, rows, tile), jnp.bfloat16),
            jax.ShapeDtypeStruct((rows, tile), jnp.float32),
        ],
        compiler_params=pltpu.CompilerParams(vmem_limit_bytes=48 * 2**20),
        name="flow_step",
    )(cols.reshape(-1), low, high, inj, w, cap.reshape(-1, 1, block * tile), bus)


def inject_kernel(lo_sm, hi_sm, slow_sm, disp, bus, wind, load, inj, split):
    chunks, rows, tile = disp.shape
    tiles = inj.shape[0]
    for c in range(chunks):
        value = disp[c]
        first = value.astype(jnp.bfloat16).astype(jnp.float32)
        second = (value - first).astype(jnp.bfloat16).astype(jnp.float32)
        third = value - first - second
        split[c] = jnp.concatenate([first, second, third], axis=0).astype(jnp.bfloat16)

    def folded(sums):
        return sums[:rows] + sums[rows:2 * rows] + sums[2 * rows:]

    def outside(lanes):
        return wind[:, lanes].astype(jnp.float32) - load[:, lanes].astype(jnp.float32)

    for t in range(tiles):
        c = lo_sm[t]
        buses = lax.broadcasted_iota(jnp.int32, (tile, 2 * tile), 0) + t * tile
        here = jnp.concatenate([bus[c], bus[c + 1]], axis=1)
        onehot = jnp.where(buses == here, 1.0, 0.0).astype(jnp.bfloat16)
        left = jnp.concatenate([split[c], split[c + 1]], axis=1)
        sums = lax.dot_general(left, onehot, NT, preferred_element_type=jnp.float32)
        placed = folded(sums) + outside(slice(t * tile, (t + 1) * tile))
        inj[t] = placed.astype(jnp.bfloat16)

    @pl.when(slow_sm[0] > 0)
    def _():
        def one(t, carry):
            buses = lax.broadcasted_iota(jnp.int32, (tile, tile), 0) + t * tile

            def more(c, sums):
                onehot = jnp.where(buses == bus[c], 1.0, 0.0).astype(jnp.bfloat16)
                return sums + lax.dot_general(split[c], onehot, NT, preferred_element_type=jnp.float32)

            zero = jnp.zeros((3 * rows, tile), jnp.float32)
            sums = lax.fori_loop(lo_sm[t], hi_sm[t] + 1, more, zero)
            lanes = pl.ds(pl.multiple_of(t * tile, tile), tile)
            inj[t] = (folded(sums) + outside(lanes)).astype(jnp.bfloat16)
            return carry

        lax.fori_loop(0, tiles, one, 0)


def injected(disp, bus, wind, load, low, high, slow):
    chunks, rows, tile = disp.shape
    tiles = low.shape[0]
    smem = pl.BlockSpec(memory_space=pltpu.SMEM)
    vmem = pl.BlockSpec(memory_space=pltpu.VMEM)
    return pl.pallas_call(
        inject_kernel,
        in_specs=[smem] * 3 + [vmem] * 4,
        out_specs=vmem,
        out_shape=jax.ShapeDtypeStruct((tiles, rows, tile), jnp.bfloat16),
        scratch_shapes=[pltpu.VMEM((chunks, 3 * rows, tile), jnp.bfloat16)],
        name="inject",
    )(low, high, slow, disp, bus, wind, load)


def on_device(areas, wind, load, ptdf_tiles, tile_cols, line_cap, gen_bus, gen_data, prob_weight):
    scen_local, hours, bus_local = wind.shape
    gens = gen_bus.shape[0]
    tile = ptdf_tiles.shape[2]
    rows = scen_local * hours
    chunks = gens // tile
    tiles = bus_local // tile
    buses = bus_local * areas
    first_bus = lax.axis_index("area") * bus_local

    index = jnp.arange(gens, dtype=jnp.int32)
    ahead = (gen_bus[None, :] < gen_bus[:, None]) | (
        (gen_bus[None, :] == gen_bus[:, None]) & (index[None, :] < index[:, None])
    )
    rank = jnp.sum(ahead.astype(jnp.int32), axis=1)
    order = (rank[:, None] == index[None, :]).astype(jnp.float32)
    per_gen = jnp.concatenate([gen_data, gen_bus.astype(jnp.float32)[None]], axis=0)
    per_gen = jnp.dot(per_gen, order, precision=HIGH, preferred_element_type=jnp.float32)
    bus_sorted = jnp.round(per_gen[4]).astype(jnp.int32)
    data = per_gen[:4].reshape(4, chunks, 1, tile)
    linear, quadratic, fixed_cost, capacity = data[0], data[1], data[2], data[3]
    step_gen = 1.0 / (quadratic + penalty + 2.0)

    bus_local_sorted = bus_sorted - first_bus
    starts = jnp.sum(
        (bus_local_sorted[None, :] < (jnp.arange(tiles + 1, dtype=jnp.int32) * tile)[:, None]).astype(jnp.int32), axis=1
    )
    low = jnp.minimum(starts[:-1] // tile, chunks - 2)
    high = (starts[1:] - 1) // tile
    slow = jnp.any(high > low + 1).astype(jnp.int32)[None]
    bus_chunks = bus_local_sorted.reshape(chunks, 1, tile)

    bus_all = lax.all_gather(bus_sorted, "area", axis=0, tiled=True).reshape(-1, 1, tile)
    group_low = bus_all[:, 0, 0] // tile
    group_high = bus_all[:, 0, -1] // tile

    total = lax.psum(jnp.sum(prob_weight.astype(jnp.float32)), "scen")
    probs = jnp.repeat(prob_weight.astype(jnp.float32) / total, hours)[None, :, None]

    shape = (chunks, rows, tile)
    commit = jnp.full(shape, 0.5, jnp.float32)
    dispatch = jnp.zeros(shape, jnp.float32) + 0.25 * capacity
    comm_mean = jnp.full((chunks, hours, tile), 0.5, jnp.float32)
    disp_mean = jnp.zeros((chunks, hours, tile), jnp.float32) + 0.25 * capacity
    w_comm = jnp.zeros(shape, jnp.float32)
    w_disp = jnp.zeros(shape, jnp.float32)
    wind_rows = wind.reshape(rows, bus_local)
    load_rows = jnp.tile(load, (scen_local, 1))
    flow = None
    for round_index in range(ITERS):
        comm_rows = jnp.tile(comm_mean, (1, scen_local, 1))
        disp_rows = jnp.tile(disp_mean, (1, scen_local, 1))
        for step_index in range(STEPS):
            injection = injected(dispatch, bus_chunks, wind_rows, load_rows, low, high, slow)
            whole = lax.all_gather(injection, "area", axis=0, tiled=True)
            flow, partial_price, imbalance = flows_and_prices(
                whole, ptdf_tiles, tile_cols, line_cap, bus_all, group_low, group_high
            )
            pieces = lax.all_to_all(
                partial_price.reshape(areas, chunks, rows, tile), "area", 0, 0
            )
            price_gen = jnp.sum(pieces.astype(jnp.float32), axis=0)
            grad = (
                linear
                + quadratic * dispatch
                + flow_weight * price_gen
                + imbalance[None] / buses
                + w_disp
                + penalty * (dispatch - disp_rows)
            )
            commit = jnp.clip(
                commit
                - commit_step
                * (fixed_cost - dispatch / capacity + w_comm + penalty * (commit - comm_rows)),
                0.0,
                1.0,
            )
            dispatch = jnp.clip(dispatch - step_gen * grad, 0.0, capacity * commit)
        both = jnp.stack([probs * commit, probs * dispatch])
        both = jnp.sum(both.reshape(2, chunks, scen_local, hours, tile), axis=2)
        comm_mean, disp_mean = lax.psum(both, "scen")
        w_comm = w_comm + penalty * (commit - jnp.tile(comm_mean, (1, scen_local, 1)))
        w_disp = w_disp + penalty * (dispatch - jnp.tile(disp_mean, (1, scen_local, 1)))

    outs = jnp.concatenate([comm_mean, disp_mean, dispatch], axis=1)
    outs = jnp.moveaxis(outs, 0, 1).reshape(-1, gens)
    outs = lax.dot_general(
        outs, order, NT, precision=HIGH, preferred_element_type=jnp.float32
    )
    return (
        outs[:hours],
        outs[hours:2 * hours],
        outs[2 * hours:].reshape(scen_local, hours, gens),
        flow.reshape(scen_local, hours, -1),
    )


def solution(mesh):
    placed = (
        P("scen", None, "area"),
        P(None, "area"),
        P("area", None, None, None),
        P("area", None),
        P("area"),
        P("area"),
        P(None, "area"),
        P("scen"),
    )
    return jax.shard_map(
        functools.partial(on_device, mesh.shape["area"]),
        mesh=mesh,
        in_specs=placed,
        out_specs=(
            P(None, "area"),
            P(None, "area"),
            P("scen", None, "area"),
            P("scen", None, "area"),
        ),
        check_vma=False,
    )
```

```python
import functools
import jax
import jax.numpy as jnp
from jax import lax
from jax.experimental import pallas as pl
from jax.experimental.pallas import tpu as pltpu
from jax.sharding import PartitionSpec as P

ITERS = 2
STEPS = 2

penalty = 1.0
flow_weight = 0.25
commit_step = 0.5

SPAN = 8
NT = (((1,), (1,)), ((), ()))
HIGH = lax.Precision.HIGHEST


def flow_kernel(cols_sm, lo_sm, hi_sm, inj, w, cap, bus, flow, price, imb, acc):
    step = pl.program_id(0)
    block, slots, tile, _ = w.shape
    tiles = inj.shape[0]

    @pl.when(step == 0)
    def _():
        acc[...] = jnp.zeros_like(acc)

        def add(t, sums):
            return tuple(s + inj[t * 4 + i].astype(jnp.float32) for i, s in enumerate(sums))

        zero = jnp.zeros(imb.shape, jnp.float32)
        parts = lax.fori_loop(0, tiles // 4, add, (zero,) * 4)
        total = parts[0] + parts[1] + parts[2] + parts[3]
        imb[...] = jnp.broadcast_to(jnp.sum(total, axis=1, keepdims=True), imb.shape)

    flows = []
    cols = []
    for kk in range(block):
        base = (step * block + kk) * slots
        own = [cols_sm[base + z] for z in range(slots)]
        picked = jnp.concatenate([inj[c] for c in own], axis=1)
        wide = jnp.concatenate([w[kk, z] for z in range(slots)], axis=1)
        flows.append(lax.dot_general(picked, wide, NT, preferred_element_type=jnp.float32))
        cols.append(own)
    contribs = []
    for kk in range(block):
        value = flows[kk]
        flow[:, kk * tile:(kk + 1) * tile] = value
        limit = cap[0, :, kk * tile:(kk + 1) * tile]
        excess = (value - jnp.clip(value, -limit, limit)).astype(jnp.bfloat16)
        wide = jnp.concatenate([w[kk, z] for z in range(slots)], axis=1)
        contribs.append(jnp.dot(excess, wide, preferred_element_type=jnp.float32))
    for kk in range(block):
        for z in range(slots):
            c = cols[kk][z]
            acc[c] = acc[c] + contribs[kk][:, z * tile:(z + 1) * tile]

    @pl.when(step == pl.num_programs(0) - 1)
    def _():
        def one(j, carry):
            where = jnp.broadcast_to(bus[j], imb.shape)
            own_tile = where // tile
            lane = where - own_tile * tile

            def pick(t, found):
                values = acc[t].astype(jnp.bfloat16).astype(jnp.float32)
                got = jnp.take_along_axis(values, lane, axis=1, mode="promise_in_bounds")
                return jnp.where(own_tile == t, got, found)

            found = jnp.zeros(imb.shape, jnp.float32)
            low = lo_sm[j]
            for i in range(SPAN):
                found = pick(jnp.minimum(low + i, tiles - 1), found)
            found = lax.fori_loop(low + SPAN, hi_sm[j] + 1, pick, found)
            price[j] = found.astype(jnp.bfloat16)
            return carry

        lax.fori_loop(0, bus.shape[0], one, 0)


def flows_and_prices(inj, w, cols, cap, bus, low, high, block=2):
    tiles, rows, tile = inj.shape
    lines, slots = w.shape[0], w.shape[1]
    block = block if lines % block == 0 else 1
    groups = bus.shape[0]
    return pl.pallas_call(
        flow_kernel,
        grid_spec=pltpu.PrefetchScalarGridSpec(
            num_scalar_prefetch=3,
            grid=(lines // block,),
            in_specs=[
                pl.BlockSpec((tiles, rows, tile), lambda k, *_: (0, 0, 0)),
                pl.BlockSpec((block, slots, tile, tile), lambda k, *_: (k, 0, 0, 0)),
                pl.BlockSpec((1, 1, block * tile), lambda k, *_: (k, 0, 0)),
                pl.BlockSpec((groups, 1, tile), lambda k, *_: (0, 0, 0)),
            ],
            out_specs=[
                pl.BlockSpec((rows, block * tile), lambda k, *_: (0, k)),
                pl.BlockSpec((groups, rows, tile), lambda k, *_: (0, 0, 0)),
                pl.BlockSpec((rows, tile), lambda k, *_: (0, 0)),
            ],
            scratch_shapes=[pltpu.VMEM((tiles, rows, tile), jnp.float32)],
        ),
        out_shape=[
            jax.ShapeDtypeStruct((rows, lines * tile), jnp.float32),
            jax.ShapeDtypeStruct((groups, rows, tile), jnp.bfloat16),
            jax.ShapeDtypeStruct((rows, tile), jnp.float32),
        ],
        compiler_params=pltpu.CompilerParams(vmem_limit_bytes=48 * 2**20),
        name="flow_step",
    )(cols.reshape(-1), low, high, inj, w, cap.reshape(-1, 1, block * tile), bus)


def inject_kernel(lo_sm, hi_sm, slow_sm, disp, bus, wind, load, inj, split):
    chunks, rows, tile = disp.shape
    tiles = inj.shape[0]
    for c in range(chunks):
        value = disp[c]
        first = value.astype(jnp.bfloat16).astype(jnp.float32)
        second = (value - first).astype(jnp.bfloat16).astype(jnp.float32)
        third = value - first - second
        split[c] = jnp.concatenate([first, second, third], axis=0).astype(jnp.bfloat16)

    def folded(sums):
        return sums[:rows] + sums[rows:2 * rows] + sums[2 * rows:]

    def outside(lanes):
        return wind[:, lanes].astype(jnp.float32) - load[:, lanes].astype(jnp.float32)

    for t in range(tiles):
        c = lo_sm[t]
        buses = lax.broadcasted_iota(jnp.int32, (tile, 2 * tile), 0) + t * tile
        here = jnp.concatenate([bus[c], bus[c + 1]], axis=1)
        onehot = jnp.where(buses == here, 1.0, 0.0).astype(jnp.bfloat16)
        left = jnp.concatenate([split[c], split[c + 1]], axis=1)
        sums = lax.dot_general(left, onehot, NT, preferred_element_type=jnp.float32)
        placed = folded(sums) + outside(slice(t * tile, (t + 1) * tile))
        inj[t] = placed.astype(jnp.bfloat16)

    @pl.when(slow_sm[0] > 0)
    def _():
        def one(t, carry):
            buses = lax.broadcasted_iota(jnp.int32, (tile, tile), 0) + t * tile

            def more(c, sums):
                onehot = jnp.where(buses == bus[c], 1.0, 0.0).astype(jnp.bfloat16)
                return sums + lax.dot_general(split[c], onehot, NT, preferred_element_type=jnp.float32)

            zero = jnp.zeros((3 * rows, tile), jnp.float32)
            sums = lax.fori_loop(lo_sm[t], hi_sm[t] + 1, more, zero)
            lanes = pl.ds(pl.multiple_of(t * tile, tile), tile)
            inj[t] = (folded(sums) + outside(lanes)).astype(jnp.bfloat16)
            return carry

        lax.fori_loop(0, tiles, one, 0)


def injected(disp, bus, wind, load, low, high, slow):
    chunks, rows, tile = disp.shape
    tiles = low.shape[0]
    smem = pl.BlockSpec(memory_space=pltpu.SMEM)
    vmem = pl.BlockSpec(memory_space=pltpu.VMEM)
    return pl.pallas_call(
        inject_kernel,
        in_specs=[smem] * 3 + [vmem] * 4,
        out_specs=vmem,
        out_shape=jax.ShapeDtypeStruct((tiles, rows, tile), jnp.bfloat16),
        scratch_shapes=[pltpu.VMEM((chunks, 3 * rows, tile), jnp.bfloat16)],
        name="inject",
    )(low, high, slow, disp, bus, wind, load)


MESH = pl.DeviceIdType.MESH
VMEM = pl.BlockSpec(memory_space=pltpu.VMEM)


def greet(axis, peers):
    barrier = pltpu.get_barrier_semaphore()
    for peer in peers:
        pl.semaphore_signal(barrier, inc=1, device_id={axis: peer}, device_id_type=MESH)
    pl.semaphore_wait(barrier, len(peers))


def sent(axis, peer, src, dst, send, recv):
    copy = pltpu.make_async_remote_copy(
        src_ref=src, dst_ref=dst, send_sem=send, recv_sem=recv, device_id={axis: peer}, device_id_type=MESH
    )
    copy.start()
    return copy


def remote(kernel, out, args, sems, scratch, ident, name):
    return pl.pallas_call(
        kernel,
        in_specs=[VMEM] * len(args),
        out_specs=VMEM,
        out_shape=out,
        scratch_shapes=list(scratch) + [pltpu.SemaphoreType.DMA((k,)) for k in sems],
        compiler_params=pltpu.CompilerParams(collective_id=ident, has_side_effects=True),
        name=name,
    )(*args)


def gather_kernel(axis, n, x, out, send, recv):
    me = lax.axis_index(axis)
    peers = [lax.rem(me + i, n) for i in range(1, n)]
    greet(axis, peers)
    copies = [sent(axis, peer, x, out.at[me], send.at[i], recv.at[i]) for i, peer in enumerate(peers)]
    out[me] = x[...]
    for copy in copies:
        copy.wait()


def gathered(x, axis, n, ident):
    out = jax.ShapeDtypeStruct((n,) + x.shape, x.dtype)
    return remote(functools.partial(gather_kernel, axis, n), out, [x], [n - 1] * 2, [], ident, "gather")


def exchange_kernel(axis, n, x, out, landed, send, recv):
    me = lax.axis_index(axis)
    peers = [lax.rem(me + i, n) for i in range(1, n)]
    greet(axis, peers)
    copies = [
        sent(axis, peer, x.at[peer], landed.at[i], send.at[i], recv.at[i]) for i, peer in enumerate(peers)
    ]
    total = x[me].astype(jnp.float32)
    for i, copy in enumerate(copies):
        copy.wait_recv()
        total = total + landed[i].astype(jnp.float32)
    out[...] = total
    for copy in copies:
        copy.wait_send()


def exchanged(x, axis, n, ident):
    out = jax.ShapeDtypeStruct(x.shape[1:], jnp.float32)
    scratch = [pltpu.VMEM((n - 1,) + x.shape[1:], x.dtype)]
    return remote(functools.partial(exchange_kernel, axis, n), out, [x], [n - 1] * 2, scratch, ident, "exchange")


def mean_kernel(axis, n, x, out, landed, mine, send, recv, send_out, recv_out):
    me = lax.axis_index(axis)
    peers = [lax.rem(me + i, n) for i in range(1, n)]
    greet(axis, peers)
    copies = [
        sent(axis, peer, x.at[peer], landed.at[i], send.at[i], recv.at[i]) for i, peer in enumerate(peers)
    ]
    total = x[me]
    for i, copy in enumerate(copies):
        copy.wait_recv()
        total = total + landed[i]
    mine[...] = total
    out[me] = total
    later = [
        sent(axis, peer, mine, out.at[me], send_out.at[i], recv_out.at[i]) for i, peer in enumerate(peers)
    ]
    for copy in copies:
        copy.wait_send()
    for copy in later:
        copy.wait()


def summed(x, axis, n, ident):
    size = x.size // 128
    if n < 2 or size % (8 * n):
        return lax.psum(x, axis)
    parts = x.reshape(n, size // n, 128)
    scratch = [
        pltpu.VMEM((n - 1,) + parts.shape[1:], x.dtype),
        pltpu.VMEM(parts.shape[1:], x.dtype),
    ]
    out = jax.ShapeDtypeStruct(parts.shape, x.dtype)
    kernel = functools.partial(mean_kernel, axis, n)
    return remote(kernel, out, [parts], [n - 1] * 4, scratch, ident, "mean").reshape(x.shape)


def spread_kernel(axis, n, parts, x, out, *sems):
    me = lax.axis_index(axis)
    chips = n // 2
    chip, core = me // 2, lax.rem(me, 2)
    sibling = me + 1 - 2 * core
    tiles = x.shape[0] // parts
    across = [lax.rem(chip + j, chips) * 2 + core for j in range(1, chips)]
    greet(axis, [sibling] + across)
    near_send, near_recv, far_send, far_recv, on_send, on_recv = sems
    copies = []
    pieces = [pl.ds(p * tiles, tiles) for p in range(parts)]
    for p, piece in enumerate(pieces):
        for j, peer in enumerate(across):
            k = j * parts + p
            copies.append(sent(axis, peer, x.at[piece], out.at[me, piece], far_send.at[k], far_recv.at[k]))
    near = sent(axis, sibling, x, out.at[me], near_send.at[0], near_recv.at[0])
    out[me] = x[...]
    passed = []
    for p, piece in enumerate(pieces):
        for j in range(1, chips):
            k = (j - 1) * parts + p
            copies[p * (chips - 1) + j - 1].wait_recv()
            origin = lax.rem(chip + chips - j, chips) * 2 + core
            landed = out.at[origin, piece]
            passed.append(sent(axis, sibling, landed, landed, on_send.at[k], on_recv.at[k]))
    near.wait()
    for copy in copies:
        copy.wait_send()
    for copy in passed:
        copy.wait()


def spread(x, axis, n, ident):
    parts = 4 if x.shape[0] % 4 == 0 else 1
    if n % 2 or n < 4:
        return gathered(x, axis, n, ident).reshape(-1, *x.shape[1:])
    out = jax.ShapeDtypeStruct((n,) + x.shape, x.dtype)
    far = (n // 2 - 1) * parts
    kernel = functools.partial(spread_kernel, axis, n, parts)
    return remote(kernel, out, [x], [1, 1, far, far, far, far], [], ident, "spread").reshape(-1, *x.shape[1:])


def on_device(areas, scens, wind, load, ptdf_tiles, tile_cols, line_cap, gen_bus, gen_data, prob_weight):
    scen_local, hours, bus_local = wind.shape
    gens = gen_bus.shape[0]
    tile = ptdf_tiles.shape[2]
    rows = scen_local * hours
    chunks = gens // tile
    tiles = bus_local // tile
    buses = bus_local * areas
    first_bus = lax.axis_index("area") * bus_local

    index = jnp.arange(gens, dtype=jnp.int32)
    ahead = (gen_bus[None, :] < gen_bus[:, None]) | (
        (gen_bus[None, :] == gen_bus[:, None]) & (index[None, :] < index[:, None])
    )
    rank = jnp.sum(ahead.astype(jnp.int32), axis=1)
    order = (rank[:, None] == index[None, :]).astype(jnp.float32)
    per_gen = jnp.concatenate([gen_data, gen_bus.astype(jnp.float32)[None]], axis=0)
    per_gen = jnp.dot(per_gen, order, precision=HIGH, preferred_element_type=jnp.float32)
    bus_sorted = jnp.round(per_gen[4]).astype(jnp.int32)
    data = per_gen[:4].reshape(4, chunks, 1, tile)
    linear, quadratic, fixed_cost, capacity = data[0], data[1], data[2], data[3]
    step_gen = 1.0 / (quadratic + penalty + 2.0)

    bus_local_sorted = bus_sorted - first_bus
    starts = jnp.sum(
        (bus_local_sorted[None, :] < (jnp.arange(tiles + 1, dtype=jnp.int32) * tile)[:, None]).astype(jnp.int32), axis=1
    )
    low = jnp.minimum(starts[:-1] // tile, chunks - 2)
    high = (starts[1:] - 1) // tile
    slow = jnp.any(high > low + 1).astype(jnp.int32)[None]
    bus_chunks = bus_local_sorted.reshape(chunks, 1, tile)

    bus_all = gathered(bus_sorted.reshape(chunks, tile), "area", areas, 0).reshape(-1, 1, tile)
    group_low = bus_all[:, 0, 0] // tile
    group_high = bus_all[:, 0, -1] // tile

    own = jnp.broadcast_to(jnp.sum(prob_weight.astype(jnp.float32)), (8, 128))
    total = jnp.sum(gathered(own, "scen", scens, 1)[:, 0, 0])
    probs = jnp.repeat(prob_weight.astype(jnp.float32) / total, hours)[None, :, None]

    shape = (chunks, rows, tile)
    commit = jnp.full(shape, 0.5, jnp.float32)
    dispatch = jnp.zeros(shape, jnp.float32) + 0.25 * capacity
    comm_mean = jnp.full((chunks, hours, tile), 0.5, jnp.float32)
    disp_mean = jnp.zeros((chunks, hours, tile), jnp.float32) + 0.25 * capacity
    w_comm = jnp.zeros(shape, jnp.float32)
    w_disp = jnp.zeros(shape, jnp.float32)
    wind_rows = wind.reshape(rows, bus_local)
    load_rows = jnp.tile(load, (scen_local, 1))
    flow = None
    for round_index in range(ITERS):
        comm_rows = jnp.tile(comm_mean, (1, scen_local, 1))
        disp_rows = jnp.tile(disp_mean, (1, scen_local, 1))
        for step_index in range(STEPS):
            injection = injected(dispatch, bus_chunks, wind_rows, load_rows, low, high, slow)
            whole = spread(injection, "area", areas, 2)
            flow, partial_price, imbalance = flows_and_prices(
                whole, ptdf_tiles, tile_cols, line_cap, bus_all, group_low, group_high
            )
            price_gen = exchanged(partial_price.reshape(areas, chunks, rows, tile), "area", areas, 3)
            grad = (
                linear
                + quadratic * dispatch
                + flow_weight * price_gen
                + imbalance[None] / buses
                + w_disp
                + penalty * (dispatch - disp_rows)
            )
            commit = jnp.clip(
                commit
                - commit_step
                * (fixed_cost - dispatch / capacity + w_comm + penalty * (commit - comm_rows)),
                0.0,
                1.0,
            )
            dispatch = jnp.clip(dispatch - step_gen * grad, 0.0, capacity * commit)
        both = jnp.stack([probs * commit, probs * dispatch])
        both = jnp.sum(both.reshape(2, chunks, scen_local, hours, tile), axis=2)
        comm_mean, disp_mean = summed(both, "scen", scens, 4)
        w_comm = w_comm + penalty * (commit - jnp.tile(comm_mean, (1, scen_local, 1)))
        w_disp = w_disp + penalty * (dispatch - jnp.tile(disp_mean, (1, scen_local, 1)))

    outs = jnp.concatenate([comm_mean, disp_mean, dispatch], axis=1)
    outs = jnp.moveaxis(outs, 0, 1).reshape(-1, gens)
    outs = lax.dot_general(
        outs, order, NT, precision=HIGH, preferred_element_type=jnp.float32
    )
    return (
        outs[:hours],
        outs[hours:2 * hours],
        outs[2 * hours:].reshape(scen_local, hours, gens),
        flow.reshape(scen_local, hours, -1),
    )


def solution(mesh):
    placed = (
        P("scen", None, "area"),
        P(None, "area"),
        P("area", None, None, None),
        P("area", None),
        P("area"),
        P("area"),
        P(None, "area"),
        P("scen"),
    )
    return jax.shard_map(
        functools.partial(on_device, mesh.shape["area"], mesh.shape["scen"]),
        mesh=mesh,
        in_specs=placed,
        out_specs=(
            P(None, "area"),
            P(None, "area"),
            P("scen", None, "area"),
            P("scen", None, "area"),
        ),
        check_vma=False,
    )
```

```python
import functools
import jax
import jax.numpy as jnp
from jax import lax
from jax.experimental import pallas as pl
from jax.experimental.pallas import tpu as pltpu
from jax.sharding import PartitionSpec as P

ITERS = 2
STEPS = 2

penalty = 1.0
flow_weight = 0.25
commit_step = 0.5

SPAN = 8
NT = (((1,), (1,)), ((), ()))
HIGH = lax.Precision.HIGHEST


def flow_kernel(cols_sm, lo_sm, hi_sm, inj, w, cap, bus, flow, price, imb, acc):
    step = pl.program_id(0)
    block, slots, tile, _ = w.shape
    tiles = inj.shape[0]

    @pl.when(step == 0)
    def _():
        acc[...] = jnp.zeros_like(acc)

        def add(t, sums):
            return tuple(s + inj[t * 4 + i].astype(jnp.float32) for i, s in enumerate(sums))

        zero = jnp.zeros(imb.shape, jnp.float32)
        parts = lax.fori_loop(0, tiles // 4, add, (zero,) * 4)
        total = parts[0] + parts[1] + parts[2] + parts[3]
        imb[...] = jnp.broadcast_to(jnp.sum(total, axis=1, keepdims=True), imb.shape)

    flows = []
    cols = []
    for kk in range(block):
        base = (step * block + kk) * slots
        own = [cols_sm[base + z] for z in range(slots)]
        picked = jnp.concatenate([inj[c] for c in own], axis=1)
        wide = jnp.concatenate([w[kk, z] for z in range(slots)], axis=1)
        flows.append(lax.dot_general(wide, picked, NT, preferred_element_type=jnp.float32).T)
        cols.append(own)
    contribs = []
    for kk in range(block):
        value = flows[kk]
        flow[:, kk * tile:(kk + 1) * tile] = value
        limit = cap[0, :, kk * tile:(kk + 1) * tile]
        excess = (value - jnp.clip(value, -limit, limit)).astype(jnp.bfloat16)
        wide = jnp.concatenate([w[kk, z] for z in range(slots)], axis=1)
        contribs.append(jnp.dot(excess, wide, preferred_element_type=jnp.float32))
    for kk in range(block):
        for z in range(slots):
            c = cols[kk][z]
            acc[c] = acc[c] + contribs[kk][:, z * tile:(z + 1) * tile]

    @pl.when(step == pl.num_programs(0) - 1)
    def _():
        def one(j, carry):
            where = jnp.broadcast_to(bus[j], imb.shape)
            own_tile = where // tile
            lane = where - own_tile * tile

            def pick(t, found):
                values = acc[t].astype(jnp.bfloat16).astype(jnp.float32)
                got = jnp.take_along_axis(values, lane, axis=1, mode="promise_in_bounds")
                return jnp.where(own_tile == t, got, found)

            found = jnp.zeros(imb.shape, jnp.float32)
            low = lo_sm[j]
            for i in range(SPAN):
                found = pick(jnp.minimum(low + i, tiles - 1), found)
            found = lax.fori_loop(low + SPAN, hi_sm[j] + 1, pick, found)
            price[j] = found.astype(jnp.bfloat16)
            return carry

        lax.fori_loop(0, bus.shape[0], one, 0)


def flows_and_prices(inj, w, cols, cap, bus, low, high, block=4):
    tiles, rows, tile = inj.shape
    lines, slots = w.shape[0], w.shape[1]
    block = block if lines % block == 0 else 1
    groups = bus.shape[0]
    return pl.pallas_call(
        flow_kernel,
        grid_spec=pltpu.PrefetchScalarGridSpec(
            num_scalar_prefetch=3,
            grid=(lines // block,),
            in_specs=[
                pl.BlockSpec((tiles, rows, tile), lambda k, *_: (0, 0, 0)),
                pl.BlockSpec((block, slots, tile, tile), lambda k, *_: (k, 0, 0, 0)),
                pl.BlockSpec((1, 1, block * tile), lambda k, *_: (k, 0, 0)),
                pl.BlockSpec((groups, 1, tile), lambda k, *_: (0, 0, 0)),
            ],
            out_specs=[
                pl.BlockSpec((rows, block * tile), lambda k, *_: (0, k)),
                pl.BlockSpec((groups, rows, tile), lambda k, *_: (0, 0, 0)),
                pl.BlockSpec((rows, tile), lambda k, *_: (0, 0)),
            ],
            scratch_shapes=[pltpu.VMEM((tiles, rows, tile), jnp.float32)],
        ),
        out_shape=[
            jax.ShapeDtypeStruct((rows, lines * tile), jnp.float32),
            jax.ShapeDtypeStruct((groups, rows, tile), jnp.bfloat16),
            jax.ShapeDtypeStruct((rows, tile), jnp.float32),
        ],
        compiler_params=pltpu.CompilerParams(vmem_limit_bytes=48 * 2**20),
        name="flow_step",
    )(cols.reshape(-1), low, high, inj, w, cap.reshape(-1, 1, block * tile), bus)


def inject_kernel(lo_sm, hi_sm, slow_sm, disp, bus, wind, load, inj, split):
    chunks, rows, tile = disp.shape
    tiles = inj.shape[0]
    for c in range(chunks):
        value = disp[c]
        first = value.astype(jnp.bfloat16).astype(jnp.float32)
        second = (value - first).astype(jnp.bfloat16).astype(jnp.float32)
        third = value - first - second
        split[c] = jnp.concatenate([first, second, third], axis=0).astype(jnp.bfloat16)

    def folded(sums):
        return sums[:rows] + sums[rows:2 * rows] + sums[2 * rows:]

    def outside(lanes):
        return wind[:, lanes].astype(jnp.float32) - load[:, lanes].astype(jnp.float32)

    for t in range(tiles):
        c = lo_sm[t]
        buses = lax.broadcasted_iota(jnp.int32, (tile, 2 * tile), 0) + t * tile
        here = jnp.concatenate([bus[c], bus[c + 1]], axis=1)
        onehot = jnp.where(buses == here, 1.0, 0.0).astype(jnp.bfloat16)
        left = jnp.concatenate([split[c], split[c + 1]], axis=1)
        sums = lax.dot_general(left, onehot, NT, preferred_element_type=jnp.float32)
        placed = folded(sums) + outside(slice(t * tile, (t + 1) * tile))
        inj[t] = placed.astype(jnp.bfloat16)

    @pl.when(slow_sm[0] > 0)
    def _():
        def one(t, carry):
            buses = lax.broadcasted_iota(jnp.int32, (tile, tile), 0) + t * tile

            def more(c, sums):
                onehot = jnp.where(buses == bus[c], 1.0, 0.0).astype(jnp.bfloat16)
                return sums + lax.dot_general(split[c], onehot, NT, preferred_element_type=jnp.float32)

            zero = jnp.zeros((3 * rows, tile), jnp.float32)
            sums = lax.fori_loop(lo_sm[t], hi_sm[t] + 1, more, zero)
            lanes = pl.ds(pl.multiple_of(t * tile, tile), tile)
            inj[t] = (folded(sums) + outside(lanes)).astype(jnp.bfloat16)
            return carry

        lax.fori_loop(0, tiles, one, 0)


def injected(disp, bus, wind, load, low, high, slow):
    chunks, rows, tile = disp.shape
    tiles = low.shape[0]
    smem = pl.BlockSpec(memory_space=pltpu.SMEM)
    vmem = pl.BlockSpec(memory_space=pltpu.VMEM)
    return pl.pallas_call(
        inject_kernel,
        in_specs=[smem] * 3 + [vmem] * 4,
        out_specs=vmem,
        out_shape=jax.ShapeDtypeStruct((tiles, rows, tile), jnp.bfloat16),
        scratch_shapes=[pltpu.VMEM((chunks, 3 * rows, tile), jnp.bfloat16)],
        name="inject",
    )(low, high, slow, disp, bus, wind, load)


MESH = pl.DeviceIdType.MESH
VMEM = pl.BlockSpec(memory_space=pltpu.VMEM)


def greet(axis, peers):
    barrier = pltpu.get_barrier_semaphore()
    for peer in peers:
        pl.semaphore_signal(barrier, inc=1, device_id={axis: peer}, device_id_type=MESH)
    pl.semaphore_wait(barrier, len(peers))


def sent(axis, peer, src, dst, send, recv):
    copy = pltpu.make_async_remote_copy(
        src_ref=src, dst_ref=dst, send_sem=send, recv_sem=recv, device_id={axis: peer}, device_id_type=MESH
    )
    copy.start()
    return copy


def remote(kernel, out, args, sems, scratch, ident, name):
    return pl.pallas_call(
        kernel,
        in_specs=[VMEM] * len(args),
        out_specs=VMEM,
        out_shape=out,
        scratch_shapes=list(scratch) + [pltpu.SemaphoreType.DMA((k,)) for k in sems],
        compiler_params=pltpu.CompilerParams(collective_id=ident, has_side_effects=True),
        name=name,
    )(*args)


def gather_kernel(axis, n, x, out, send, recv):
    me = lax.axis_index(axis)
    peers = [lax.rem(me + i, n) for i in range(1, n)]
    greet(axis, peers)
    copies = [sent(axis, peer, x, out.at[me], send.at[i], recv.at[i]) for i, peer in enumerate(peers)]
    out[me] = x[...]
    for copy in copies:
        copy.wait()


def gathered(x, axis, n, ident):
    out = jax.ShapeDtypeStruct((n,) + x.shape, x.dtype)
    return remote(functools.partial(gather_kernel, axis, n), out, [x], [n - 1] * 2, [], ident, "gather")


def exchange_kernel(axis, n, x, out, landed, send, recv):
    me = lax.axis_index(axis)
    peers = [lax.rem(me + i, n) for i in range(1, n)]
    greet(axis, peers)
    copies = [
        sent(axis, peer, x.at[peer], landed.at[i], send.at[i], recv.at[i]) for i, peer in enumerate(peers)
    ]
    total = x[me].astype(jnp.float32)
    for i, copy in enumerate(copies):
        copy.wait_recv()
        total = total + landed[i].astype(jnp.float32)
    out[...] = total
    for copy in copies:
        copy.wait_send()


def exchanged(x, axis, n, ident):
    out = jax.ShapeDtypeStruct(x.shape[1:], jnp.float32)
    scratch = [pltpu.VMEM((n - 1,) + x.shape[1:], x.dtype)]
    return remote(functools.partial(exchange_kernel, axis, n), out, [x], [n - 1] * 2, scratch, ident, "exchange")


class Mean:
    def __init__(self, axis, n, x, out, landed, mine, send, recv, send_out, recv_out):
        self.me = lax.axis_index(axis)
        self.axis, self.x, self.out, self.landed, self.mine = axis, x, out, landed, mine
        self.sems = send, recv, send_out, recv_out
        self.peers = [lax.rem(self.me + i, n) for i in range(1, n)]
        self.greeted = axis, self.peers

    def start(self):
        send, recv = self.sems[:2]
        self.copies = [
            sent(self.axis, peer, self.x.at[peer], self.landed.at[i], send.at[i], recv.at[i])
            for i, peer in enumerate(self.peers)
        ]

    def middle(self):
        send, recv = self.sems[2:]
        total = self.x[self.me]
        for i, copy in enumerate(self.copies):
            copy.wait_recv()
            total = total + self.landed[i]
        self.mine[...] = total
        self.out[self.me] = total
        self.later = [
            sent(self.axis, peer, self.mine, self.out.at[self.me], send.at[i], recv.at[i])
            for i, peer in enumerate(self.peers)
        ]

    def finish(self):
        for copy in self.copies:
            copy.wait_send()
        for copy in self.later:
            copy.wait()


class Spread:
    def __init__(self, axis, n, parts, x, out, *sems):
        self.me = lax.axis_index(axis)
        self.axis, self.parts, self.x, self.out, self.sems = axis, parts, x, out, sems
        self.chips = n // 2
        self.chip, self.core = self.me // 2, lax.rem(self.me, 2)
        self.sibling = self.me + 1 - 2 * self.core
        self.across = [lax.rem(self.chip + j, self.chips) * 2 + self.core for j in range(1, self.chips)]
        self.greeted = axis, [self.sibling] + self.across
        tiles = x.shape[0] // parts
        self.pieces = [pl.ds(p * tiles, tiles) for p in range(parts)]

    def start(self):
        near_send, near_recv, far_send, far_recv = self.sems[:4]
        me, x, out = self.me, self.x, self.out
        self.copies = []
        for p, piece in enumerate(self.pieces):
            for j, peer in enumerate(self.across):
                k = j * self.parts + p
                self.copies.append(
                    sent(self.axis, peer, x.at[piece], out.at[me, piece], far_send.at[k], far_recv.at[k])
                )
        self.near = sent(self.axis, self.sibling, x, out.at[me], near_send.at[0], near_recv.at[0])
        out[me] = x[...]

    def middle(self):
        on_send, on_recv = self.sems[4:]
        chips = self.chips
        self.passed = []
        for p, piece in enumerate(self.pieces):
            for j in range(1, chips):
                k = (j - 1) * self.parts + p
                self.copies[p * (chips - 1) + j - 1].wait_recv()
                origin = lax.rem(self.chip + chips - j, chips) * 2 + self.core
                landed = self.out.at[origin, piece]
                self.passed.append(
                    sent(self.axis, self.sibling, landed, landed, on_send.at[k], on_recv.at[k])
                )

    def finish(self):
        self.near.wait()
        for copy in self.copies:
            copy.wait_send()
        for copy in self.passed:
            copy.wait()


def greet_all(groups):
    barrier = pltpu.get_barrier_semaphore()
    for axis, peers in groups:
        for peer in peers:
            pl.semaphore_signal(barrier, inc=1, device_id={axis: peer}, device_id_type=MESH)
    pl.semaphore_wait(barrier, sum(len(peers) for _, peers in groups))


def transfers_kernel(moves, *refs):
    count = len(moves)
    sources, outs, rest = refs[:count], refs[count:2 * count], refs[2 * count:]
    runs = []
    for (make, own, _, _, _), x, out in zip(moves, sources, outs):
        runs.append(make(x, out, *rest[:own]))
        rest = rest[own:]
    greet_all([run.greeted for run in runs])
    for phase in ("start", "middle", "finish"):
        for run in runs:
            getattr(run, phase)()


def transferred(moves, ident, name):
    args = [move[2] for move in moves]
    return pl.pallas_call(
        functools.partial(transfers_kernel, [move[:2] + (None,) * 3 for move in moves]),
        in_specs=[VMEM] * len(args),
        out_specs=[VMEM] * len(args),
        out_shape=[move[3] for move in moves],
        scratch_shapes=[entry for move in moves for entry in move[4]],
        compiler_params=pltpu.CompilerParams(collective_id=ident, has_side_effects=True),
        name=name,
    )(*args)


def dma(*counts):
    return [pltpu.SemaphoreType.DMA((k,)) for k in counts]


def mean_move(x, axis, n):
    scratch = [pltpu.VMEM((n - 1,) + x.shape[1:], x.dtype), pltpu.VMEM(x.shape[1:], x.dtype)]
    scratch += dma(n - 1, n - 1, n - 1, n - 1)
    return functools.partial(Mean, axis, n), len(scratch), x, jax.ShapeDtypeStruct(x.shape, x.dtype), scratch


def spread_move(x, axis, n):
    parts = 4 if x.shape[0] % 4 == 0 else 1
    far = (n // 2 - 1) * parts
    scratch = dma(1, 1, far, far, far, far)
    out = jax.ShapeDtypeStruct((n,) + x.shape, x.dtype)
    return functools.partial(Spread, axis, n, parts), len(scratch), x, out, scratch


def in_parts(both, weight, n):
    size = both.size // 128
    if n < 2 or size % (8 * n):
        return None
    parts = both.reshape(n, size // n, 128)
    return jnp.concatenate([parts, jnp.broadcast_to(weight, (n, 8, 128))], axis=1)


def from_parts(parts, shape):
    return (parts[:, :-8] / parts[:, -8:-7]).reshape(shape)


def averaged(both, weight, axis, n, ident):
    parts = in_parts(both, weight, n)
    if parts is None:
        return lax.psum(both, axis) / lax.psum(weight, axis)
    (out,) = transferred([mean_move(parts, axis, n)], ident, "mean")
    return from_parts(out, both.shape)


def spread(x, axis, n, ident):
    if n % 2 or n < 4:
        return gathered(x, axis, n, ident).reshape(-1, *x.shape[1:])
    (out,) = transferred([spread_move(x, axis, n)], ident, "spread")
    return out.reshape(-1, *x.shape[1:])


def spread_and_averaged(x, axis, n, both, weight, other, m, idents):
    parts = in_parts(both, weight, m)
    if parts is None or n % 2 or n < 4:
        return spread(x, axis, n, idents[0]), averaged(both, weight, other, m, idents[1])
    mean, out = transferred([mean_move(parts, other, m), spread_move(x, axis, n)], idents[2], "spread_mean")
    return out.reshape(-1, *x.shape[1:]), from_parts(mean, both.shape)


def on_device(areas, scens, wind, load, ptdf_tiles, tile_cols, line_cap, gen_bus, gen_data, prob_weight):
    scen_local, hours, bus_local = wind.shape
    gens = gen_bus.shape[0]
    tile = ptdf_tiles.shape[2]
    rows = scen_local * hours
    chunks = gens // tile
    tiles = bus_local // tile
    buses = bus_local * areas
    first_bus = lax.axis_index("area") * bus_local

    index = jnp.arange(gens, dtype=jnp.int32)
    ahead = (gen_bus[None, :] < gen_bus[:, None]) | (
        (gen_bus[None, :] == gen_bus[:, None]) & (index[None, :] < index[:, None])
    )
    rank = jnp.sum(ahead.astype(jnp.int32), axis=1)
    order = (rank[:, None] == index[None, :]).astype(jnp.float32)
    per_gen = jnp.concatenate([gen_data, gen_bus.astype(jnp.float32)[None]], axis=0)
    per_gen = jnp.dot(per_gen, order, precision=HIGH, preferred_element_type=jnp.float32)
    bus_sorted = jnp.round(per_gen[4]).astype(jnp.int32)
    data = per_gen[:4].reshape(4, chunks, 1, tile)
    linear, quadratic, fixed_cost, capacity = data[0], data[1], data[2], data[3]
    step_gen = 1.0 / (quadratic + penalty + 2.0)

    bus_local_sorted = bus_sorted - first_bus
    starts = jnp.sum(
        (bus_local_sorted[None, :] < (jnp.arange(tiles + 1, dtype=jnp.int32) * tile)[:, None]).astype(jnp.int32), axis=1
    )
    low = jnp.minimum(starts[:-1] // tile, chunks - 2)
    high = (starts[1:] - 1) // tile
    slow = jnp.any(high > low + 1).astype(jnp.int32)[None]
    bus_chunks = bus_local_sorted.reshape(chunks, 1, tile)

    bus_all = gathered(bus_sorted.reshape(chunks, tile), "area", areas, 0).reshape(-1, 1, tile)
    group_low = bus_all[:, 0, 0] // tile
    group_high = bus_all[:, 0, -1] // tile

    weight = prob_weight.astype(jnp.float32)
    weights = jnp.repeat(weight, hours)[None, :, None]
    weight = jnp.sum(weight)

    shape = (chunks, rows, tile)
    commit = jnp.full(shape, 0.5, jnp.float32)
    dispatch = jnp.zeros(shape, jnp.float32) + 0.25 * capacity
    comm_mean = jnp.full((chunks, hours, tile), 0.5, jnp.float32)
    disp_mean = jnp.zeros((chunks, hours, tile), jnp.float32) + 0.25 * capacity
    w_comm = jnp.zeros(shape, jnp.float32)
    w_disp = jnp.zeros(shape, jnp.float32)
    wind_rows = wind.reshape(rows, bus_local)
    load_rows = jnp.tile(load, (scen_local, 1))
    flow = None
    both = None
    for round_index in range(ITERS):
        for step_index in range(STEPS):
            injection = injected(dispatch, bus_chunks, wind_rows, load_rows, low, high, slow)
            if both is None:
                whole = spread(injection, "area", areas, 2)
            else:
                whole, means = spread_and_averaged(
                    injection, "area", areas, both, weight, "scen", scens, (2, 4, 5)
                )
                comm_mean, disp_mean = means
                w_comm = w_comm + penalty * (commit - jnp.tile(comm_mean, (1, scen_local, 1)))
                w_disp = w_disp + penalty * (dispatch - jnp.tile(disp_mean, (1, scen_local, 1)))
                both = None
            comm_rows = jnp.tile(comm_mean, (1, scen_local, 1))
            disp_rows = jnp.tile(disp_mean, (1, scen_local, 1))
            flow, partial_price, imbalance = flows_and_prices(
                whole, ptdf_tiles, tile_cols, line_cap, bus_all, group_low, group_high
            )
            price_gen = exchanged(partial_price.reshape(areas, chunks, rows, tile), "area", areas, 3)
            grad = (
                linear
                + quadratic * dispatch
                + flow_weight * price_gen
                + imbalance[None] / buses
                + w_disp
                + penalty * (dispatch - disp_rows)
            )
            commit = jnp.clip(
                commit
                - commit_step
                * (fixed_cost - dispatch / capacity + w_comm + penalty * (commit - comm_rows)),
                0.0,
                1.0,
            )
            dispatch = jnp.clip(dispatch - step_gen * grad, 0.0, capacity * commit)
        both = jnp.stack([weights * commit, weights * dispatch])
        both = jnp.sum(both.reshape(2, chunks, scen_local, hours, tile), axis=2)
    comm_mean, disp_mean = averaged(both, weight, "scen", scens, 4)

    outs = jnp.concatenate([comm_mean, disp_mean, dispatch], axis=1)
    outs = jnp.moveaxis(outs, 0, 1).reshape(-1, gens)
    outs = lax.dot_general(
        outs, order, NT, precision=HIGH, preferred_element_type=jnp.float32
    )
    return (
        outs[:hours],
        outs[hours:2 * hours],
        outs[2 * hours:].reshape(scen_local, hours, gens),
        flow.reshape(scen_local, hours, -1),
    )


def solution(mesh):
    placed = (
        P("scen", None, "area"),
        P(None, "area"),
        P("area", None, None, None),
        P("area", None),
        P("area"),
        P("area"),
        P(None, "area"),
        P("scen"),
    )
    return jax.shard_map(
        functools.partial(on_device, mesh.shape["area"], mesh.shape["scen"]),
        mesh=mesh,
        in_specs=placed,
        out_specs=(
            P(None, "area"),
            P(None, "area"),
            P("scen", None, "area"),
            P("scen", None, "area"),
        ),
        check_vma=False,
    )
```
